512 devices in a mesh: ep: 128 (over x, z, core), dp: 4 (over y).
Axes of the slice: x: 4, y: 4, z: 16, core: 2. Of those that a mesh axis runs over, the one named last changes fastest.
Arguments:
- hidden: bfloat16 [8, 128, 256, 768], P('dp', 'ep'), parts along dimension 0, may hold values from -6 to 6
- down_weight: bfloat16 [128, 768, 2048], P('ep'), may hold values from -0.21875 to 0.21875
- routes: int32 [8, 2048, 8], P('dp', 'ep'), parts along dimension 0, may hold values from 0 to 127, all different within a row; in each aligned block of 16 rows (0 to 15, 16 to 31, ..., all dimensions but the last counted through in order) at most 2 rows name the same one
- route_weight: float32 [8, 2048, 8], P('dp', 'ep'), parts along dimension 0, may hold values from 0.03 to 0.4
- residual: bfloat16 [8, 2048, 2048], P('dp', 'ep'), parts along dimension 0, may hold values from -6 to 6
Outputs:
- mixed: bfloat16 [8, 2048, 2048], P('dp', 'ep'), parts along dimension 0
The draws below stay inside these ranges and needn't reach their ends.
There are 4 independent parts, one for each index of `dp`. The reference program is written for one: setup_inputs(seed, part) draws one part's arguments, and reference() takes and returns one part's arrays. A program takes and returns all parts, laid end to end along the dimension named above; an argument that names none is the same for every part. Nothing has to cross between parts.
Inputs may be any that keep to these rules, and one draw needn't show every extreme that they name: `routes`: each row names 8 different experts. In each micro-batch the 16 rows of one device name no expert more than 2 times, and in every draw some device's rows name some expert exactly 2 times.
All inputs are finite; a program needn't handle non-finite values.
Results may differ from the reference program's by a relative error of at most 0.0031.
Values may be sent and summed in bfloat16 or wider, within the bound.
No kernel may reach another device: no remote copies, remote signals or barrier semaphores. Data moves between devices by JAX's collectives and lax.ppermute only.
A program may use at most 64 MiB of HBM per device.

```python
import math
import jax
import jax.numpy as jnp
import numpy as np
from jax import lax

D = 2048
H = 768
TOP = 8
BATCHES = 2
MB_TOK = 16
EXPERTS = 128
MOST = 2
SLOTS = 256
TOKENS = 2048
N_EP = 128


def shard_levels(own_key, shape, split, smallest, top_value):
    loudness = 1.0
    for dim, shards_of in split:
        steps = jax.random.uniform(jax.random.fold_in(jax.random.fold_in(own_key, 6), dim), (shards_of,), jnp.float32, smallest / len(split), top_value / len(split))
        loudness = loudness * jnp.repeat(jnp.exp(steps), shape[dim] // shards_of).reshape((-1,) + (1,) * (len(shape) - 1 - dim))
    return loudness


def deal_out(key, own, number, rows, number_of, top, limit, slope):
    ranking = jax.random.permutation(key, number_of)
    heavy_load, common = portions_of(number_of, rows * top, limit, slope, True), portions_of(number_of, rows * top, limit, slope, False)
    places = jnp.arange(number_of)

    def named(lengths, rotation):
        used = int((lengths > 0).sum())
        fixed = max(1, used // 4)
        moved = fixed + (places - fixed + rotation * (used - fixed)) % max(1, number_of - fixed)
        return jnp.zeros((number_of,), jnp.int32).at[ranking[jnp.where(places < fixed, places, moved)]].set(jnp.asarray(lengths, jnp.int32))

    lengths = jnp.where(number % 4 == 0, named(heavy_load, number // 4), named(common, number - number // 4 - 1))
    mixed = jax.random.permutation(jax.random.fold_in(own, 3), number_of)
    source_of, sink = mixed[0:number_of // 2 * 2:2], mixed[1:number_of // 2 * 2:2]
    slack = jnp.minimum(lengths[source_of] - 1, limit - lengths[sink]) // 2
    slack = jnp.where((source_of == ranking[0]) | (sink == ranking[0]) | (lengths[sink] == 0), 0, jnp.maximum(slack, 0))
    moved = jax.random.randint(jax.random.fold_in(own, 4), (number_of // 2,), 0, 1 << 20) % (slack + 1)
    lengths = lengths.at[source_of].add(-moved).at[sink].add(moved)
    items = jnp.searchsorted(jnp.cumsum(lengths), jnp.arange(rows * top), side="right").astype(jnp.int32)
    listing = items.reshape(top, rows).T
    listing = listing[jax.random.permutation(jax.random.fold_in(own, 1), rows)]
    rotation = jax.random.randint(jax.random.fold_in(own, 2), (rows, 1), 0, top)
    return jnp.take_along_axis(listing, (jnp.arange(top)[None, :] + rotation) % top, axis=1)


def portions_of(number_of, total, reach, lean, full):
    portions = [(1 << 20) // math.isqrt(standing ** lean) + 1 for standing in range(1, number_of + 1)]
    largest = reach if full else min(reach, max(-(-total // number_of), total * portions[0] // sum(portions)))
    least = 1 if total - largest >= number_of - 1 else 0
    holding, rest = [largest] + [least] * (number_of - 1), total - largest - least * (number_of - 1)
    while rest > 0:
        movable = [i for i in range(1, number_of) if holding[i] < largest] or [i for i in range(1, number_of) if holding[i] < reach]
        pool, remaining = sum([portions[i] for i in movable]), rest
        for i in movable:
            extra = min(reach - holding[i], max(1, remaining * portions[i] // pool), rest)
            holding[i] = holding[i] + extra
            rest = rest - extra
    return np.array(holding)


def scatter_about(key, dims, spread, limit, cuts=(), held_as=jnp.bfloat16):
    result = jax.random.normal(key, dims, jnp.float32) * spread
    if len(cuts) > 0:
        result = shard_levels(key, dims, cuts, -0.22, 0.18) * result
    return jnp.clip(result, min=-limit, max=limit).astype(held_as)


def setup_inputs(seed: int = 0, part: int = 0) -> dict:
    streams_of = jax.random.split(jax.random.key(seed), 6)
    own_keys = jax.random.split(jax.random.fold_in(streams_of[5], part), 6)
    hidden = scatter_about(own_keys[0], (BATCHES, EXPERTS, SLOTS, H), 1.0, 6.0, ((1, 128),))
    down_weight = scatter_about(streams_of[1], (EXPERTS, H, D), H ** -0.5, 0.21875, ((0, 128),))
    routes_keys = jax.random.split(jax.random.fold_in(own_keys[2], 1), BATCHES * TOKENS // MB_TOK)
    routes_turns = jax.random.permutation(jax.random.fold_in(own_keys[2], 3), BATCHES * TOKENS // MB_TOK)
    routes = jax.vmap(lambda own, number: deal_out(jax.random.fold_in(own_keys[2], 2), own, number, MB_TOK, EXPERTS, TOP, MOST, 3))(routes_keys, routes_turns).reshape((BATCHES, TOKENS, TOP))
    route_weight = jnp.clip(jnp.exp(math.log(0.4) - 2.5902672 * jax.random.uniform(own_keys[3], (BATCHES, TOKENS, TOP), jnp.float32) ** shard_levels(own_keys[3], (BATCHES, TOKENS, TOP), ((1, 128),), -0.2, 0.2)), 0.03, 0.4)
    residual = scatter_about(own_keys[4], (BATCHES, TOKENS, D), 1.0, 6.0, ((1, 128),))
    return {"hidden": hidden, "down_weight": down_weight, "routes": routes, "route_weight": route_weight, "residual": residual}


def placement_of(routes_one):
    labels = jnp.arange(EXPERTS, dtype=jnp.int32)
    picked = jnp.sum((routes_one[:, :, None] == labels[None, None, :]).astype(jnp.int32), axis=1, dtype=jnp.int32)
    blocks = picked.reshape(N_EP, MB_TOK, EXPERTS)
    counts = jnp.sum(blocks, axis=1, dtype=jnp.int32)
    offsets = jnp.cumsum(counts, axis=0, dtype=jnp.int32) - counts
    before = jnp.cumsum(blocks, axis=1, dtype=jnp.int32) - blocks
    places = (offsets[:, None, :] + before).reshape(TOKENS, EXPERTS)
    position = jnp.take_along_axis(places, routes_one, axis=1).astype(jnp.int32)
    return position, jnp.sum(counts, axis=0, dtype=jnp.int32)


def one_batch(hidden_one, down_weight, routes_one, weight_one, residual_one):
    position, totals = placement_of(routes_one)
    token_ids = jnp.broadcast_to(jnp.arange(TOKENS, dtype=jnp.int32)[:, None], routes_one.shape)
    owners = jnp.zeros((EXPERTS, SLOTS), jnp.int32).at[routes_one, position].set(token_ids)
    shares = jnp.zeros((EXPERTS, SLOTS), jnp.float32).at[routes_one, position].set(weight_one)

    def visit_expert(summed, inputs):
        rows_in, matrix, owner_ids, share_row, live_rows = inputs

        def add_block(block_index, summed_in):
            begin_at = (block_index * 8).astype(jnp.int32)
            segment = lax.dynamic_slice_in_dim(rows_in, begin_at, 8, 0)
            product = jnp.dot(segment, matrix, preferred_element_type=jnp.float32).astype(jnp.bfloat16)
            product = lax.optimization_barrier(product).astype(jnp.float32)
            targets = lax.dynamic_slice_in_dim(owner_ids, begin_at, 8, 0)
            factor = lax.dynamic_slice_in_dim(share_row, begin_at, 8, 0)
            return summed_in.at[targets].add(factor[:, None] * product)

        block_count = ((live_rows + 7) // 8).astype(jnp.int32)
        return lax.fori_loop(jnp.int32(0), block_count, add_block, summed), None

    summed = jnp.zeros((TOKENS, D), jnp.float32)
    summed, _ = lax.scan(visit_expert, summed, (hidden_one, down_weight, owners, shares, totals))
    return (residual_one.astype(jnp.float32) + summed).astype(jnp.bfloat16)


def reference(hidden, down_weight, routes, route_weight, residual):
    results = [one_batch(hidden[batch_index], down_weight, routes[batch_index], route_weight[batch_index], residual[batch_index]) for batch_index in range(BATCHES)]
    return jnp.stack(results, axis=0)
```

```python
import jax
import jax.numpy as jnp
from jax import lax
from jax.experimental import pallas as pl
from jax.experimental.pallas import tpu as pltpu
from jax.sharding import Mesh
from jax.sharding import PartitionSpec as P

BF = jnp.bfloat16
F32 = jnp.float32
I32 = jnp.int32

X, Z, C = 4, 16, 2
NL = 2
NH = Z // NL
M = X * NL * C
B, R, MOST = 2, 16, 2
J = NH * B
SEND = M * J * MOST
DENSE = J * R
LANES = 128
RP = LANES // (M * MOST)
RQ = B * R // RP
GROUP = ("x", "zl", "c")


def iota(shape, dim):
    return lax.broadcasted_iota(I32, shape, dim)


def mm(a, b):
    return jnp.dot(a, b, preferred_element_type=F32)


def expert_of(member, high):
    x = member // (NL * C)
    rest = member % (NL * C)
    return (x * NH + high) * (NL * C) + rest


def pack_kernel(routes_ref, weight_ref, out_ref):
    rows = B * R
    routes = routes_ref[...]
    weight = weight_ref[...]
    row = iota((rows, rows), 0)
    col = iota((rows, rows), 1)
    earlier = ((row // R == col // R) & (col < row)).astype(BF)
    lane = iota((rows, LANES), 1)
    line = iota((rows, LANES), 0)
    member = (lane % (M * MOST)) // MOST
    keep = (line % RP) == lane // (M * MOST)
    for high in range(NH):
        expert = expert_of(member, high)
        total = jnp.zeros((rows, LANES), F32)
        hit = jnp.zeros((rows, LANES), F32)
        for k in range(routes.shape[1]):
            same = routes[:, k : k + 1] == expert
            total = total + jnp.where(same, weight[:, k : k + 1], 0.0)
            hit = hit + jnp.where(same, 1.0, 0.0)
        rank = mm(earlier, hit.astype(BF))
        good = keep & (rank == (lane % MOST).astype(F32))
        value = jnp.where(good, total, 0.0)
        out_ref[high] = jnp.sum(value.reshape(RQ, RP, LANES), axis=1)


def count_kernel(packed_ref, out_ref):
    packed = packed_ref[...].reshape(NH * RQ, LANES)
    used = jnp.where(packed != 0.0, 1.0, 0.0).astype(BF)
    per = RQ // B
    spread = (iota((NH * RQ, LANES), 0) // per == iota((NH * RQ, LANES), 1)).astype(BF)
    by_lane = lax.dot_general(
        used, spread, (((0,), (0,)), ((), ())), preferred_element_type=F32
    ).astype(BF)
    pick = (iota((M, LANES), 0) == (iota((M, LANES), 1) % (M * MOST)) // MOST).astype(BF)
    counts = mm(pick, by_lane)
    out_ref[...] = jnp.broadcast_to(counts[:, None, :], out_ref.shape)


def keys(index, member_of, j_of):
    member = member_of(index)
    j = j_of(index)
    return expert_of(member, j // B), j % B


def select_kernel(counts_ref, rows_ref, out_ref, pick_ref):
    @pl.when(pl.program_id(0) == 0)
    def _():
        counts = counts_ref[:, 0, :].astype(BF)
        tile = (iota((LANES, M * J), 0) == iota((LANES, M * J), 1) % J).astype(BF)
        wide = mm(counts, tile)
        own = iota((M, M * J), 0) == iota((M, M * J), 1) // J
        flat = jnp.sum(jnp.where(own, wide, 0.0), axis=0, keepdims=True)
        dst = iota((SEND, 1), 0)
        s_row, b_row = keys(dst, lambda i: i // (J * MOST), lambda i: (i % (J * MOST)) // MOST)
        src = iota((1, M * J), 1)
        s_col, b_col = keys(src, lambda i: i // J, lambda i: i % J)
        before = (b_row == b_col) & (s_col < s_row)
        offset = jnp.sum(jnp.where(before, flat, 0.0), axis=1, keepdims=True)
        slots = rows_ref.shape[0] // B
        at = offset.astype(I32) + dst % MOST + b_row * slots
        pick_ref[...] = (at == iota((SEND, rows_ref.shape[0]), 1)).astype(BF)

    out_ref[...] = mm(pick_ref[...], rows_ref[...]).astype(BF)


def combine_kernel(packed_ref, rows_ref, out_ref, high_ref, low_ref):
    @pl.when(pl.program_id(0) == 0)
    def _():
        packed = packed_ref[...].reshape(NH * RQ, LANES)
        spread = (iota((DENSE, NH * RQ), 0) // RP == iota((DENSE, NH * RQ), 1)).astype(BF)
        keep = iota((DENSE, LANES), 0) % RP == iota((DENSE, LANES), 1) // (M * MOST)
        lane = iota((LANES, SEND), 0) % (M * MOST)
        col = iota((LANES, SEND), 1)
        place = (lane // MOST == col // (J * MOST)) & (lane % MOST == col % MOST)
        place = place.astype(BF)
        mine = iota((DENSE, SEND), 0) // R == (iota((DENSE, SEND), 1) % (J * MOST)) // MOST
        first = packed.astype(BF)
        second = (packed - first.astype(F32)).astype(BF)
        for part, ref in ((first, high_ref), (second, low_ref)):
            lines = jnp.where(keep, mm(spread, part), 0.0).astype(BF)
            ref[...] = jnp.where(mine, mm(lines, place), 0.0).astype(BF)

    rows = rows_ref[...]
    out_ref[...] = (mm(high_ref[...], rows) + mm(low_ref[...], rows)).astype(BF)


def shards(hidden, down_weight, routes, route_weight, residual):
    width = down_weight.shape[2]
    slots = hidden.shape[2]
    top = routes.shape[2]
    tile = 512
    packed = pl.pallas_call(
        pack_kernel,
        out_shape=jax.ShapeDtypeStruct((NH, RQ, LANES), F32),
        name="pack",
    )(routes.reshape(B * R, top), route_weight.reshape(B * R, top))
    packed = lax.all_to_all(packed, "zh", 0, 0, tiled=True)
    counts = pl.pallas_call(
        count_kernel,
        out_shape=jax.ShapeDtypeStruct((M, 8, LANES), F32),
        name="count",
    )(packed)
    counts = lax.all_to_all(counts, GROUP, 0, 0, tiled=True)
    produced = jnp.dot(
        hidden.reshape(B * slots, -1), down_weight[0], preferred_element_type=F32
    ).astype(BF)
    sending = pl.pallas_call(
        select_kernel,
        grid=(width // tile,),
        in_specs=[
            pl.BlockSpec((M, 8, LANES), lambda i: (0, 0, 0)),
            pl.BlockSpec((B * slots, tile), lambda i: (0, i)),
        ],
        out_specs=pl.BlockSpec((SEND, tile), lambda i: (0, i)),
        out_shape=jax.ShapeDtypeStruct((SEND, width), BF),
        scratch_shapes=[pltpu.VMEM((SEND, B * slots), BF)],
        name="select",
    )(counts, produced)
    near = lax.all_to_all(sending.reshape(M, J * MOST, width), GROUP, 0, 0, tiled=True)
    dense = pl.pallas_call(
        combine_kernel,
        grid=(width // tile,),
        in_specs=[
            pl.BlockSpec((NH, RQ, LANES), lambda i: (0, 0, 0)),
            pl.BlockSpec((SEND, tile), lambda i: (0, i)),
        ],
        out_specs=pl.BlockSpec((DENSE, tile), lambda i: (0, i)),
        out_shape=jax.ShapeDtypeStruct((DENSE, width), BF),
        scratch_shapes=[pltpu.VMEM((DENSE, SEND), BF), pltpu.VMEM((DENSE, SEND), BF)],
        name="combine",
    )(packed, near.reshape(SEND, width))
    far = lax.all_to_all(dense.reshape(NH, B * R, width), "zh", 0, 0, tiled=True)
    mixed = residual.reshape(B * R, width).astype(F32) + jnp.sum(far.astype(F32), axis=0)
    return mixed.astype(BF).reshape(residual.shape)


def solution(mesh):
    fine = Mesh(mesh.devices.reshape(X, NH, NL, C, -1), ("x", "zh", "zl", "c", "dp"))
    ep = ("x", "zh", "zl", "c")
    in_specs = (
        P("dp", ep, None, None),
        P(ep, None, None),
        P("dp", ep, None),
        P("dp", ep, None),
        P("dp", ep, None),
    )
    out_specs = P("dp", ep, None)
    return jax.shard_map(shards, mesh=fine, in_specs=in_specs, out_specs=out_specs, check_vma=False)
```

```python
import jax
import jax.numpy as jnp
from jax import lax
from jax.experimental import pallas as pl
from jax.experimental.pallas import tpu as pltpu
from jax.sharding import Mesh
from jax.sharding import PartitionSpec as P

BF = jnp.bfloat16
F32 = jnp.float32
I32 = jnp.int32

X, Z, C = 4, 16, 2
NL = 2
NH = Z // NL
M = X * NL * C
B, R, MOST = 2, 16, 2
PAIRS = M * NH
TILE = 512
LANES = 128
RP = LANES // (M * MOST)
RQ = B * R // RP
GROUP = ("x", "zl", "c")


def iota(shape, dim):
    return lax.broadcasted_iota(I32, shape, dim)


def mm(a, b):
    return jnp.dot(a, b, preferred_element_type=F32)


def expert_of(member, high):
    x = member // (NL * C)
    rest = member % (NL * C)
    return (x * NH + high) * (NL * C) + rest


def turned(block):
    eye = (iota((R, R), 0) == iota((R, R), 1)).astype(F32)
    return lax.dot_general(
        eye,
        block,
        (((1,), (1,)), ((), ())),
        precision=lax.Precision.HIGHEST,
        preferred_element_type=F32,
    )


def pack_kernel(routes_ref, weight_ref, out_ref):
    rows = B * R
    routes = jnp.concatenate([turned(routes_ref[b].astype(F32)) for b in range(B)], axis=0)
    weight = jnp.concatenate([turned(weight_ref[b]) for b in range(B)], axis=0)
    row = iota((rows, rows), 0)
    col = iota((rows, rows), 1)
    earlier = ((row // R == col // R) & (col < row)).astype(BF)
    lane = iota((rows, LANES), 1)
    line = iota((rows, LANES), 0)
    member = (lane % (M * MOST)) // MOST
    keep = (line % RP) == lane // (M * MOST)
    for high in range(NH):
        expert = expert_of(member, high).astype(F32)
        total = jnp.zeros((rows, LANES), F32)
        hit = jnp.zeros((rows, LANES), F32)
        for k in range(routes.shape[1]):
            same = routes[:, k : k + 1] == expert
            total = total + jnp.where(same, weight[:, k : k + 1], 0.0)
            hit = hit + jnp.where(same, 1.0, 0.0)
        rank = mm(earlier, hit.astype(BF))
        good = keep & (rank == (lane % MOST).astype(F32))
        value = jnp.where(good, total, 0.0)
        out_ref[high] = jnp.sum(value.reshape(RQ, RP, LANES), axis=1)


def count_kernel(packed_ref, out_ref):
    packed = packed_ref[...].reshape(NH * RQ, LANES)
    used = jnp.where(packed != 0.0, 1.0, 0.0).astype(BF)
    per = RQ // B
    line = iota((NH * RQ, LANES), 0)
    spread = (((line % RQ) // per) * NH + line // RQ == iota((NH * RQ, LANES), 1)).astype(BF)
    by_lane = lax.dot_general(
        used, spread, (((0,), (0,)), ((), ())), preferred_element_type=F32
    ).astype(BF)
    pick = (iota((M, LANES), 0) == (iota((M, LANES), 1) % (M * MOST)) // MOST).astype(BF)
    out_ref[...] = mm(pick, by_lane)[:, None, :]


def select_kernel(counts_ref, rows_ref, out_ref):
    counts = counts_ref[:, 0, :].astype(BF)
    slots = rows_ref.shape[0] // B
    width = rows_ref.shape[1]
    dst = iota((PAIRS * MOST, 1), 0)
    src = iota((1, PAIRS), 1)
    s_row = expert_of(dst // (NH * MOST), (dst % (NH * MOST)) // MOST)
    s_col = expert_of(src // NH, src % NH)
    before = s_col < s_row
    own = iota((M, PAIRS), 0) == iota((M, PAIRS), 1) // NH
    for b in range(B):
        tile = iota((LANES, PAIRS), 0) == iota((LANES, PAIRS), 1) % NH + b * NH
        wide = mm(counts, tile.astype(BF))
        flat = jnp.sum(jnp.where(own, wide, 0.0), axis=0, keepdims=True)
        offset = jnp.sum(jnp.where(before, flat, 0.0), axis=1, keepdims=True)
        at = offset.astype(I32) + dst % MOST
        pick = (at == iota((PAIRS * MOST, slots), 1)).astype(BF)
        for d in range(0, width, TILE):
            rows = rows_ref[b * slots : (b + 1) * slots, d : d + TILE]
            out_ref[:, b, :, d : d + TILE] = (
                mm(pick, rows).astype(BF).reshape(M, NH * MOST, TILE)
            )


def weight_kernel(packed_ref, out_ref):
    packed = packed_ref[...].reshape(NH * RQ, LANES)
    per = RQ // B
    rows = NH * R
    cols = PAIRS * MOST
    lane = iota((LANES, cols), 0) % (M * MOST)
    col = iota((LANES, cols), 1)
    place = (lane // MOST == col // (NH * MOST)) & (lane % MOST == col % MOST)
    place = place.astype(BF)
    mine = iota((rows, cols), 0) // R == (iota((rows, cols), 1) % (NH * MOST)) // MOST
    row = iota((rows, LANES), 0)
    keep = row % RP == iota((rows, LANES), 1) // (M * MOST)
    row = iota((rows, NH * RQ), 0)
    first = packed.astype(BF)
    second = (packed - first.astype(F32)).astype(BF)
    for b in range(B):
        line = (row // R) * RQ + b * per + (row % R) // RP
        spread = (line == iota((rows, NH * RQ), 1)).astype(BF)
        for t, part in enumerate((first, second)):
            lines = jnp.where(keep, mm(spread, part), 0.0).astype(BF)
            out_ref[b, t * rows : (t + 1) * rows, :] = jnp.where(
                mine, mm(lines, place), 0.0
            ).astype(BF)


def combine_kernel(weight_ref, rows_ref, out_ref):
    width = rows_ref.shape[3]
    half = NH * R
    for b in range(B):
        weight = weight_ref[b]
        for d in range(0, width, TILE):
            rows = rows_ref[:, b, :, d : d + TILE].reshape(PAIRS * MOST, TILE)
            both = mm(weight, rows)
            out_ref[:, b, :, d : d + TILE] = (
                (both[:half] + both[half:]).astype(BF).reshape(NH, R, TILE)
            )


def kernel(body, name, shape, dtype, count):
    vmem = pl.BlockSpec(memory_space=pltpu.VMEM)
    return pl.pallas_call(
        body,
        in_specs=[vmem] * count,
        out_specs=vmem,
        out_shape=jax.ShapeDtypeStruct(shape, dtype),
        name=name,
    )


def shards(hidden, down_weight, routes, route_weight, residual):
    width = down_weight.shape[2]
    slots = hidden.shape[2]
    packed = kernel(pack_kernel, "pack", (NH, RQ, LANES), F32, 2)(
        routes.transpose(0, 2, 1), route_weight.transpose(0, 2, 1)
    )
    packed = lax.all_to_all(packed, "zh", 0, 0, tiled=True)
    counts = kernel(count_kernel, "count", (M, 1, LANES), F32, 1)(packed)
    counts = lax.all_to_all(counts, GROUP, 0, 0, tiled=True)
    produced = jnp.dot(
        hidden.reshape(B * slots, -1), down_weight[0], preferred_element_type=F32
    ).astype(BF)
    weight = kernel(weight_kernel, "weight", (B, 2 * NH * R, PAIRS * MOST), BF, 1)(packed)
    sending = kernel(select_kernel, "select", (M, B, NH * MOST, width), BF, 2)(counts, produced)
    near = lax.all_to_all(sending, GROUP, 0, 0, tiled=True)
    dense = kernel(combine_kernel, "combine", (NH, B, R, width), BF, 2)(weight, near)
    far = lax.all_to_all(dense, "zh", 0, 0, tiled=True)
    mixed = residual.astype(F32) + jnp.sum(far.astype(F32), axis=0)
    return mixed.astype(BF)


def solution(mesh):
    fine = Mesh(mesh.devices.reshape(X, NH, NL, C, -1), ("x", "zh", "zl", "c", "dp"))
    ep = ("x", "zh", "zl", "c")
    in_specs = (
        P("dp", ep, None, None),
        P(ep, None, None),
        P("dp", ep, None),
        P("dp", ep, None),
        P("dp", ep, None),
    )
    out_specs = P("dp", ep, None)
    return jax.shard_map(shards, mesh=fine, in_specs=in_specs, out_specs=out_specs, check_vma=False)
```

```python
import jax
import jax.numpy as jnp
from jax import lax
from jax.experimental import pallas as pl
from jax.experimental.pallas import tpu as pltpu
from jax.sharding import Mesh
from jax.sharding import PartitionSpec as P

BF = jnp.bfloat16
F32 = jnp.float32
I32 = jnp.int32

X, Z, C = 4, 16, 2
NL = 2
NH = Z // NL
M = X * NL * C
B, R, MOST = 2, 16, 2
PAIRS = M * NH
TILE = 512
LANES = 128
RP = LANES // (M * MOST)
RQ = B * R // RP
GROUP = ("x", "zl", "c")


def iota(shape, dim):
    return lax.broadcasted_iota(I32, shape, dim)


def mm(a, b):
    return jnp.dot(a, b, preferred_element_type=F32)


def expert_of(member, high):
    x = member // (NL * C)
    rest = member % (NL * C)
    return (x * NH + high) * (NL * C) + rest


def turned(block):
    eye = (iota((R, R), 0) == iota((R, R), 1)).astype(F32)
    return lax.dot_general(
        eye,
        block,
        (((1,), (1,)), ((), ())),
        precision=lax.Precision.HIGHEST,
        preferred_element_type=F32,
    )


def pack_kernel(routes_ref, weight_ref, out_ref):
    rows = B * R
    routes = jnp.concatenate([turned(routes_ref[b].astype(F32)) for b in range(B)], axis=0)
    weight = jnp.concatenate([turned(weight_ref[b]) for b in range(B)], axis=0)
    row = iota((rows, rows), 0)
    col = iota((rows, rows), 1)
    earlier = ((row // R == col // R) & (col < row)).astype(BF)
    lane = iota((rows, LANES), 1)
    line = iota((rows, LANES), 0)
    member = (lane % (M * MOST)) // MOST
    keep = (line % RP) == lane // (M * MOST)
    for high in range(NH):
        expert = expert_of(member, high).astype(F32)
        total = jnp.zeros((rows, LANES), F32)
        hit = jnp.zeros((rows, LANES), F32)
        for k in range(routes.shape[1]):
            same = routes[:, k : k + 1] == expert
            total = total + jnp.where(same, weight[:, k : k + 1], 0.0)
            hit = hit + jnp.where(same, 1.0, 0.0)
        rank = mm(earlier, hit.astype(BF))
        good = keep & (rank == (lane % MOST).astype(F32))
        value = jnp.where(good, total, 0.0)
        out_ref[high] = jnp.sum(value.reshape(RQ, RP, LANES), axis=1)


def count_kernel(packed_ref, out_ref):
    packed = packed_ref[...].reshape(NH * RQ, LANES)
    used = jnp.where(packed != 0.0, 1.0, 0.0).astype(BF)
    per = RQ // B
    line = iota((LANES, NH * RQ), 1)
    spread = (((line % RQ) // per) * NH + line // RQ == iota((LANES, NH * RQ), 0)).astype(BF)
    by_pair = mm(spread, used).astype(BF)
    pick = (iota((M, LANES), 0) == (iota((M, LANES), 1) % (M * MOST)) // MOST).astype(BF)
    counts = lax.dot_general(
        pick, by_pair, (((1,), (1,)), ((), ())), preferred_element_type=F32
    )
    out_ref[...] = counts[:, None, :]


def select_kernel(counts_ref, rows_ref, out_ref):
    slots = rows_ref.shape[0]
    b = pl.program_id(0)
    counts = counts_ref[:, 0, :].astype(BF)
    dst = iota((PAIRS * MOST, 1), 0)
    src = iota((1, PAIRS), 1)
    s_row = expert_of(dst // (NH * MOST), (dst % (NH * MOST)) // MOST)
    s_col = expert_of(src // NH, src % NH)
    own = iota((M, PAIRS), 0) == iota((M, PAIRS), 1) // NH
    tile = iota((LANES, PAIRS), 0) == iota((LANES, PAIRS), 1) % NH + b * NH
    wide = mm(counts, tile.astype(BF))
    flat = jnp.sum(jnp.where(own, wide, 0.0), axis=0, keepdims=True)
    offset = jnp.sum(jnp.where(s_col < s_row, flat, 0.0), axis=1, keepdims=True)
    at = offset.astype(I32) + dst % MOST
    pick = (at == iota((PAIRS * MOST, slots), 1)).astype(BF)
    for d in range(0, rows_ref.shape[1], TILE):
        out_ref[:, 0, :, d : d + TILE] = (
            mm(pick, rows_ref[:, d : d + TILE]).astype(BF).reshape(M, NH * MOST, TILE)
        )


def weight_kernel(place_ref, packed_ref, out_ref):
    packed = packed_ref[...].reshape(NH * RQ, LANES)
    per = RQ // B
    rows = NH * R
    cols = PAIRS * MOST
    lane = iota((LANES, cols), 0) % (M * MOST)
    col = iota((LANES, cols), 1)
    place = (lane // MOST == col // (NH * MOST)) & (lane % MOST == col % MOST)
    place = place.astype(BF)

    def target(row):
        step = row // R
        far = NH // 2 + jnp.where(step % 2 == 1, -((step + 1) // 2), step // 2)
        return (far + place_ref[0]) % NH

    high = target(iota((rows, 1), 0))
    mine = high == (iota((rows, cols), 1) % (NH * MOST)) // MOST
    row = iota((rows, LANES), 0)
    keep = row % RP == iota((rows, LANES), 1) // (M * MOST)
    inner = (iota((rows, 1), 0) % R) // RP
    first = packed.astype(BF)
    second = (packed - first.astype(F32)).astype(BF)
    for b in range(B):
        line = high * RQ + b * per + inner
        spread = (line == iota((rows, NH * RQ), 1)).astype(BF)
        for t, part in enumerate((first, second)):
            lines = jnp.where(keep, mm(spread, part), 0.0).astype(BF)
            out_ref[b, t] = jnp.where(mine, mm(lines, place), 0.0).astype(BF)


def summed(weight_ref, rows_ref, begin, end, d):
    rows = rows_ref[:, 0, :, d : d + TILE].reshape(PAIRS * MOST, TILE)
    low, high = begin * R, end * R
    weight = jnp.concatenate([weight_ref[0, 0, low:high, :], weight_ref[0, 1, low:high, :]], axis=0)
    both = mm(weight, rows)
    return (both[: high - low] + both[high - low :]).reshape(end - begin, R, TILE)


def far_kernel(weight_ref, rows_ref, leap_up_ref, leap_down_ref, up_ref, down_ref):
    b = pl.program_id(0)
    for d in range(0, rows_ref.shape[3], TILE):
        part = summed(weight_ref, rows_ref, 0, 3, d).astype(BF)

        @pl.when(b == 0)
        def _():
            leap_up_ref[:, d : d + TILE] = part[0]

        @pl.when(b == 1)
        def _():
            leap_down_ref[:, d : d + TILE] = part[0]

        up_ref[0, :, d : d + TILE] = part[1]
        down_ref[0, :, d : d + TILE] = part[2]


def near_kernel(weight_ref, rows_ref, up_ref, down_ref, out_ref):
    for d in range(0, rows_ref.shape[3], TILE):
        part = summed(weight_ref, rows_ref, 3, NH, d)
        up_ref[0, :, d : d + TILE] = part[2].astype(BF)
        down_ref[0, :, d : d + TILE] = part[3].astype(BF)
        out_ref[0, 0, :, d : d + TILE] = part[0]
        out_ref[1, 0, :, d : d + TILE] = part[1]
        out_ref[2, 0, :, d : d + TILE] = part[4]


def kernel(body, name, shape, dtype, count):
    vmem = pl.BlockSpec(memory_space=pltpu.VMEM)
    return pl.pallas_call(
        body,
        in_specs=[vmem] * count,
        out_specs=vmem,
        out_shape=jax.ShapeDtypeStruct(shape, dtype),
        name=name,
    )


def whole(shape):
    return pl.BlockSpec(shape, lambda b: (0,) * len(shape))


def batch(shape, dim, size=1):
    block = shape[:dim] + (size,) + shape[dim + 1 :]
    return pl.BlockSpec(block, lambda b: (0,) * dim + (b,) + (0,) * (len(shape) - dim - 1))


def shift(value, step):
    return lax.ppermute(value, "zh", [(i, (i + step) % NH) for i in range(NH)])


def shards(hidden, down_weight, routes, route_weight, residual):
    width = down_weight.shape[2]
    slots = hidden.shape[2]
    struct = jax.ShapeDtypeStruct
    packed = kernel(pack_kernel, "pack", (NH, RQ, LANES), F32, 2)(
        routes.transpose(0, 2, 1), route_weight.transpose(0, 2, 1)
    )
    packed = lax.all_to_all(packed, "zh", 0, 0, tiled=True)
    produced = jnp.dot(
        hidden.reshape(B * slots, -1), down_weight[0], preferred_element_type=F32
    ).astype(BF)
    counts = kernel(count_kernel, "count", (M, 1, LANES), F32, 1)(packed)
    counts = lax.all_to_all(counts, GROUP, 0, 0, tiled=True)
    shape = (M, B, NH * MOST, width)
    sending = pl.pallas_call(
        select_kernel,
        grid=(B,),
        in_specs=[whole(counts.shape), batch(produced.shape, 0, slots)],
        out_specs=batch(shape, 1),
        out_shape=struct(shape, BF),
        name="select",
    )(counts, produced)
    near = lax.all_to_all(sending, GROUP, 0, 0, tiled=True)
    weight = pl.pallas_call(
        weight_kernel,
        in_specs=[
            pl.BlockSpec(memory_space=pltpu.SMEM),
            pl.BlockSpec(memory_space=pltpu.VMEM),
        ],
        out_specs=pl.BlockSpec(memory_space=pltpu.VMEM),
        out_shape=struct((B, 2, NH * R, PAIRS * MOST), BF),
        name="weight",
    )(lax.axis_index("zh").astype(I32).reshape(1), packed)
    one = (R, width)
    both = (B, R, width)
    leap_up, leap_down, up, down = pl.pallas_call(
        far_kernel,
        grid=(B,),
        in_specs=[batch(weight.shape, 0), batch(near.shape, 1)],
        out_specs=[whole(one)] * 2 + [batch(both, 0)] * 2,
        out_shape=[struct(one, BF)] * 2 + [struct(both, BF)] * 2,
        name="far",
    )(weight, near)
    leap_up, leap_down = shift(leap_up, 2), shift(leap_down, -2)
    up, down = shift(up, 1), shift(down, -1)
    shape = (3, B, R, width)
    next_up, next_down, close = pl.pallas_call(
        near_kernel,
        grid=(B,),
        in_specs=[batch(weight.shape, 0), batch(near.shape, 1)],
        out_specs=[batch(both, 0)] * 2 + [batch(shape, 1)],
        out_shape=[struct(both, BF)] * 2 + [struct(shape, F32)],
        name="near",
    )(weight, near)
    next_up, next_down = shift(next_up, 1), shift(next_down, -1)
    above = close[0] + up.astype(F32)
    below = close[1] + down.astype(F32)
    first = jnp.arange(B)[:, None, None] == 0
    above = above + jnp.where(first, leap_up.astype(F32)[None], 0.0)
    below = below + jnp.where(first, 0.0, leap_down.astype(F32)[None])
    above, below = shift(above.astype(BF), 2), shift(below.astype(BF), -2)
    mixed = residual.astype(F32) + close[2]
    for part in (next_up, next_down, above, below):
        mixed = mixed + part.astype(F32)
    return mixed.astype(BF)


def solution(mesh):
    fine = Mesh(mesh.devices.reshape(X, NH, NL, C, -1), ("x", "zh", "zl", "c", "dp"))
    ep = ("x", "zh", "zl", "c")
    in_specs = (
        P("dp", ep, None, None),
        P(ep, None, None),
        P("dp", ep, None),
        P("dp", ep, None),
        P("dp", ep, None),
    )
    out_specs = P("dp", ep, None)
    return jax.shard_map(shards, mesh=fine, in_specs=in_specs, out_specs=out_specs, check_vma=False)
```

```python
import jax
import jax.numpy as jnp
from jax import lax
from jax.experimental import pallas as pl
from jax.experimental.pallas import tpu as pltpu
from jax.sharding import Mesh
from jax.sharding import PartitionSpec as P

BF = jnp.bfloat16
F32 = jnp.float32
I32 = jnp.int32

X, Z, C = 4, 16, 2
NL = 2
NH = Z // NL
M = X * NL * C
B, R, MOST = 2, 16, 2
PAIRS = M * NH
TILE = 512
LANES = 128
RP = LANES // (M * MOST)
RQ = B * R // RP
GROUP = ("x", "zl", "c")


def iota(shape, dim):
    return lax.broadcasted_iota(I32, shape, dim)


def mm(a, b):
    return jnp.dot(a, b, preferred_element_type=F32)


def expert_of(member, high):
    x = member // (NL * C)
    rest = member % (NL * C)
    return (x * NH + high) * (NL * C) + rest


def turned(block):
    eye = (iota((R, R), 0) == iota((R, R), 1)).astype(F32)
    return lax.dot_general(
        eye,
        block,
        (((1,), (1,)), ((), ())),
        precision=lax.Precision.HIGHEST,
        preferred_element_type=F32,
    )


def pack_kernel(routes_ref, weight_ref, out_ref):
    rows = B * R
    routes = jnp.concatenate([turned(routes_ref[b].astype(F32)) for b in range(B)], axis=0)
    weight = jnp.concatenate([turned(weight_ref[b]) for b in range(B)], axis=0)
    row = iota((rows, rows), 0)
    col = iota((rows, rows), 1)
    earlier = ((row // R == col // R) & (col < row)).astype(BF)
    lane = iota((rows, LANES), 1)
    line = iota((rows, LANES), 0)
    member = (lane % (M * MOST)) // MOST
    keep = (line % RP) == lane // (M * MOST)
    for high in range(NH):
        expert = expert_of(member, high).astype(F32)
        total = jnp.zeros((rows, LANES), F32)
        hit = jnp.zeros((rows, LANES), F32)
        for k in range(routes.shape[1]):
            same = routes[:, k : k + 1] == expert
            total = total + jnp.where(same, weight[:, k : k + 1], 0.0)
            hit = hit + jnp.where(same, 1.0, 0.0)
        rank = mm(earlier, hit.astype(BF))
        good = keep & (rank == (lane % MOST).astype(F32))
        value = jnp.where(good, total, 0.0)
        out_ref[high] = jnp.sum(value.reshape(RQ, RP, LANES), axis=1)


def count_kernel(packed_ref, out_ref):
    packed = packed_ref[...].reshape(NH * RQ, LANES)
    used = jnp.where(packed != 0.0, 1.0, 0.0).astype(BF)
    per = RQ // B
    line = iota((LANES, NH * RQ), 1)
    spread = (((line % RQ) // per) * NH + line // RQ == iota((LANES, NH * RQ), 0)).astype(BF)
    by_pair = mm(spread, used).astype(BF)
    pick = (iota((M, LANES), 0) == (iota((M, LANES), 1) % (M * MOST)) // MOST).astype(BF)
    counts = lax.dot_general(
        pick, by_pair, (((1,), (1,)), ((), ())), preferred_element_type=F32
    )
    out_ref[...] = counts[:, None, :]


def select_kernel(counts_ref, rows_ref, out_ref):
    slots = rows_ref.shape[0]
    b = pl.program_id(0)
    counts = counts_ref[:, 0, :].astype(BF)
    dst = iota((PAIRS * MOST, 1), 0)
    src = iota((1, PAIRS), 1)
    s_row = expert_of(dst // (NH * MOST), (dst % (NH * MOST)) // MOST)
    s_col = expert_of(src // NH, src % NH)
    own = iota((M, PAIRS), 0) == iota((M, PAIRS), 1) // NH
    tile = iota((LANES, PAIRS), 0) == iota((LANES, PAIRS), 1) % NH + b * NH
    wide = mm(counts, tile.astype(BF))
    flat = jnp.sum(jnp.where(own, wide, 0.0), axis=0, keepdims=True)
    offset = jnp.sum(jnp.where(s_col < s_row, flat, 0.0), axis=1, keepdims=True)
    at = offset.astype(I32) + dst % MOST
    pick = (at == iota((PAIRS * MOST, slots), 1)).astype(BF)
    for d in range(0, rows_ref.shape[1], TILE):
        out_ref[:, 0, :, d : d + TILE] = (
            mm(pick, rows_ref[:, d : d + TILE]).astype(BF).reshape(M, NH * MOST, TILE)
        )


def weight_kernel(place_ref, packed_ref, out_ref):
    packed = packed_ref[...].reshape(NH * RQ, LANES)
    per = RQ // B
    rows = NH * R
    cols = PAIRS * MOST
    lane = iota((LANES, cols), 0) % (M * MOST)
    col = iota((LANES, cols), 1)
    place = (lane // MOST == col // (NH * MOST)) & (lane % MOST == col % MOST)
    place = place.astype(BF)

    def target(row):
        step = row // R
        far = NH // 2 + jnp.where(step % 2 == 1, -((step + 1) // 2), step // 2)
        return (far + place_ref[0]) % NH

    high = target(iota((rows, 1), 0))
    mine = high == (iota((rows, cols), 1) % (NH * MOST)) // MOST
    row = iota((rows, LANES), 0)
    keep = row % RP == iota((rows, LANES), 1) // (M * MOST)
    inner = (iota((rows, 1), 0) % R) // RP
    first = packed.astype(BF)
    second = (packed - first.astype(F32)).astype(BF)
    for b in range(B):
        line = high * RQ + b * per + inner
        spread = (line == iota((rows, NH * RQ), 1)).astype(BF)
        for t, part in enumerate((first, second)):
            lines = jnp.where(keep, mm(spread, part), 0.0).astype(BF)
            out_ref[b, t] = jnp.where(mine, mm(lines, place), 0.0).astype(BF)


def far_kernel(weight_ref, rows_ref, leap_up_ref, leap_down_ref):
    b = pl.program_id(0)
    weight = weight_ref[0, :, :R, :].reshape(2 * R, PAIRS * MOST)
    for d in range(0, rows_ref.shape[3], TILE):
        rows = rows_ref[:, 0, :, d : d + TILE].reshape(PAIRS * MOST, TILE)
        both = mm(weight, rows)
        part = (both[:R] + both[R:]).astype(BF)

        @pl.when(b == 0)
        def _():
            leap_up_ref[:, d : d + TILE] = part

        @pl.when(b == 1)
        def _():
            leap_down_ref[:, d : d + TILE] = part


def combine_kernel(weight_ref, rows_ref, up_ref, down_ref, close_ref):
    half = NH * R - R
    weight = weight_ref[0, :, R:, :].reshape(2 * half, PAIRS * MOST)
    for d in range(0, rows_ref.shape[3], TILE):
        rows = rows_ref[:, 0, :, d : d + TILE].reshape(PAIRS * MOST, TILE)
        both = mm(weight, rows)
        part = (both[:half] + both[half:]).reshape(NH - 1, R, TILE)
        up_ref[0, 0, :, d : d + TILE] = part[0].astype(BF)
        down_ref[0, 0, :, d : d + TILE] = part[1].astype(BF)
        close_ref[0, 0, :, d : d + TILE] = part[2]
        close_ref[1, 0, :, d : d + TILE] = part[3]
        up_ref[1, 0, :, d : d + TILE] = part[4].astype(BF)
        down_ref[1, 0, :, d : d + TILE] = part[5].astype(BF)
        close_ref[2, 0, :, d : d + TILE] = part[6]


def kernel(body, name, shape, dtype, count):
    vmem = pl.BlockSpec(memory_space=pltpu.VMEM)
    return pl.pallas_call(
        body,
        in_specs=[vmem] * count,
        out_specs=vmem,
        out_shape=jax.ShapeDtypeStruct(shape, dtype),
        name=name,
    )


def whole(shape):
    return pl.BlockSpec(shape, lambda b: (0,) * len(shape))


def batch(shape, dim, size=1):
    block = shape[:dim] + (size,) + shape[dim + 1 :]
    return pl.BlockSpec(block, lambda b: (0,) * dim + (b,) + (0,) * (len(shape) - dim - 1))


def shift(value, step):
    return lax.ppermute(value, "zh", [(i, (i + step) % NH) for i in range(NH)])


def shards(hidden, down_weight, routes, route_weight, residual):
    width = down_weight.shape[2]
    slots = hidden.shape[2]
    struct = jax.ShapeDtypeStruct
    packed = kernel(pack_kernel, "pack", (NH, RQ, LANES), F32, 2)(
        routes.transpose(0, 2, 1), route_weight.transpose(0, 2, 1)
    )
    packed = lax.all_to_all(packed, "zh", 0, 0, tiled=True)
    produced = jnp.dot(
        hidden.reshape(B * slots, -1), down_weight[0], preferred_element_type=F32
    ).astype(BF)
    counts = kernel(count_kernel, "count", (M, 1, LANES), F32, 1)(packed)
    counts = jnp.maximum(lax.all_to_all(counts, GROUP, 0, 0, tiled=True), 0.0)
    shape = (M, B, NH * MOST, width)
    sending = pl.pallas_call(
        select_kernel,
        grid=(B,),
        in_specs=[whole(counts.shape), batch(produced.shape, 0, slots)],
        out_specs=batch(shape, 1),
        out_shape=struct(shape, BF),
        name="select",
    )(counts, produced)
    near = lax.all_to_all(sending, GROUP, 0, 0, tiled=True)
    weight = pl.pallas_call(
        weight_kernel,
        in_specs=[
            pl.BlockSpec(memory_space=pltpu.SMEM),
            pl.BlockSpec(memory_space=pltpu.VMEM),
        ],
        out_specs=pl.BlockSpec(memory_space=pltpu.VMEM),
        out_shape=struct((B, 2, NH * R, PAIRS * MOST), BF),
        name="weight",
    )(lax.axis_index("zh").astype(I32).reshape(1), packed)
    one = (R, width)
    both = (2, B, R, width)
    shape = (3, B, R, width)
    inputs = [batch(weight.shape, 0), batch(near.shape, 1)]
    leap_up, leap_down = pl.pallas_call(
        far_kernel,
        grid=(B,),
        in_specs=inputs,
        out_specs=[whole(one)] * 2,
        out_shape=[struct(one, BF)] * 2,
        name="far",
    )(weight, near)
    leap_up, leap_down = shift(leap_up, 2), shift(leap_down, -2)
    up, down, close = pl.pallas_call(
        combine_kernel,
        grid=(B,),
        in_specs=inputs,
        out_specs=[batch(both, 1)] * 2 + [batch(shape, 1)],
        out_shape=[struct(both, BF)] * 2 + [struct(shape, F32)],
        name="combine",
    )(weight, near)
    up, down = shift(up, 1), shift(down, -1)
    above = close[0] + up[0].astype(F32)
    below = close[1] + down[0].astype(F32)
    above = jnp.stack([above[0] + leap_up.astype(F32), above[1]]).astype(BF)
    below = jnp.stack([below[0], below[1] + leap_down.astype(F32)]).astype(BF)
    above, below = shift(above, 2), shift(below, -2)
    base = residual.astype(F32) + close[2] + up[1].astype(F32) + down[1].astype(F32)
    base = lax.optimization_barrier(base)
    return (base + above.astype(F32) + below.astype(F32)).astype(BF)


def solution(mesh):
    fine = Mesh(mesh.devices.reshape(X, NH, NL, C, -1), ("x", "zh", "zl", "c", "dp"))
    ep = ("x", "zh", "zl", "c")
    in_specs = (
        P("dp", ep, None, None),
        P(ep, None, None),
        P("dp", ep, None),
        P("dp", ep, None),
        P("dp", ep, None),
    )
    out_specs = P("dp", ep, None)
    return jax.shard_map(shards, mesh=fine, in_specs=in_specs, out_specs=out_specs, check_vma=False)
```

```python
import jax
import jax.numpy as jnp
from jax import lax
from jax.experimental import pallas as pl
from jax.experimental.pallas import tpu as pltpu
from jax.sharding import Mesh
from jax.sharding import PartitionSpec as P

BF = jnp.bfloat16
F32 = jnp.float32
I32 = jnp.int32

X, Z, C = 4, 16, 2
NL = 2
NH = Z // NL
M = X * NL * C
B, R, MOST = 2, 16, 2
PAIRS = M * NH
TILE = 1024
LANES = 128
RP = LANES // (M * MOST)
RQ = B * R // RP
GROUP = ("x", "zl", "c")


def iota(shape, dim):
    return lax.broadcasted_iota(I32, shape, dim)


def mm(a, b):
    return jnp.dot(a, b, preferred_element_type=F32)


def expert_of(member, high):
    x = member // (NL * C)
    rest = member % (NL * C)
    return (x * NH + high) * (NL * C) + rest


def turned(block):
    eye = (iota((R, R), 0) == iota((R, R), 1)).astype(F32)
    return lax.dot_general(
        eye,
        block,
        (((1,), (1,)), ((), ())),
        precision=lax.Precision.HIGHEST,
        preferred_element_type=F32,
    )


def pack_kernel(routes_ref, weight_ref, out_ref):
    rows = B * R
    routes = jnp.concatenate([turned(routes_ref[b].astype(F32)) for b in range(B)], axis=0)
    weight = jnp.concatenate([turned(weight_ref[b]) for b in range(B)], axis=0)
    row = iota((rows, rows), 0)
    col = iota((rows, rows), 1)
    earlier = ((row // R == col // R) & (col < row)).astype(BF)
    lane = iota((rows, LANES), 1)
    line = iota((rows, LANES), 0)
    member = (lane % (M * MOST)) // MOST
    keep = (line % RP) == lane // (M * MOST)
    for high in range(NH):
        expert = expert_of(member, high).astype(F32)
        total = jnp.zeros((rows, LANES), F32)
        hit = jnp.zeros((rows, LANES), F32)
        for k in range(routes.shape[1]):
            same = routes[:, k : k + 1] == expert
            total = total + jnp.where(same, weight[:, k : k + 1], 0.0)
            hit = hit + jnp.where(same, 1.0, 0.0)
        rank = mm(earlier, hit.astype(BF))
        good = keep & (rank == (lane % MOST).astype(F32))
        value = jnp.where(good, total, 0.0)
        out_ref[high] = jnp.sum(value.reshape(RQ, RP, LANES), axis=1)


def count_kernel(packed_ref, out_ref):
    packed = packed_ref[...].reshape(NH * RQ, LANES)
    used = jnp.where(packed != 0.0, 1.0, 0.0).astype(BF)
    per = RQ // B
    line = iota((LANES, NH * RQ), 1)
    spread = (((line % RQ) // per) * NH + line // RQ == iota((LANES, NH * RQ), 0)).astype(BF)
    by_pair = mm(spread, used).astype(BF)
    pick = (iota((M, LANES), 0) == (iota((M, LANES), 1) % (M * MOST)) // MOST).astype(BF)
    counts = lax.dot_general(
        pick, by_pair, (((1,), (1,)), ((), ())), preferred_element_type=F32
    )
    out_ref[...] = counts[:, None, :]


def select_kernel(counts_ref, rows_ref, out_ref):
    slots = rows_ref.shape[0]
    b = pl.program_id(0)
    counts = counts_ref[:, 0, :].astype(BF)
    dst = iota((PAIRS * MOST, 1), 0)
    src = iota((1, PAIRS), 1)
    s_row = expert_of(dst // (NH * MOST), (dst % (NH * MOST)) // MOST)
    s_col = expert_of(src // NH, src % NH)
    own = iota((M, PAIRS), 0) == iota((M, PAIRS), 1) // NH
    tile = iota((LANES, PAIRS), 0) == iota((LANES, PAIRS), 1) % NH + b * NH
    wide = mm(counts, tile.astype(BF))
    flat = jnp.sum(jnp.where(own, wide, 0.0), axis=0, keepdims=True)
    offset = jnp.sum(jnp.where(s_col < s_row, flat, 0.0), axis=1, keepdims=True)
    at = offset.astype(I32) + dst % MOST
    pick = (at == iota((PAIRS * MOST, slots), 1)).astype(BF)
    for d in range(0, rows_ref.shape[1], TILE):
        out_ref[:, 0, :, d : d + TILE] = (
            mm(pick, rows_ref[:, d : d + TILE]).astype(BF).reshape(M, NH * MOST, TILE)
        )


def weight_kernel(place_ref, packed_ref, out_ref):
    packed = packed_ref[...].reshape(NH * RQ, LANES)
    per = RQ // B
    rows = NH * R
    cols = PAIRS * MOST
    lane = iota((LANES, cols), 0) % (M * MOST)
    col = iota((LANES, cols), 1)
    place = (lane // MOST == col // (NH * MOST)) & (lane % MOST == col % MOST)
    place = place.astype(BF)

    def target(row):
        step = row // R
        far = NH // 2 + jnp.where(step % 2 == 1, -((step + 1) // 2), step // 2)
        return (far + place_ref[0]) % NH

    high = target(iota((rows, 1), 0))
    mine = high == (iota((rows, cols), 1) % (NH * MOST)) // MOST
    row = iota((rows, LANES), 0)
    keep = row % RP == iota((rows, LANES), 1) // (M * MOST)
    inner = (iota((rows, 1), 0) % R) // RP
    first = packed.astype(BF)
    second = (packed - first.astype(F32)).astype(BF)
    for b in range(B):
        line = high * RQ + b * per + inner
        spread = (line == iota((rows, NH * RQ), 1)).astype(BF)
        for t, part in enumerate((first, second)):
            lines = jnp.where(keep, mm(spread, part), 0.0).astype(BF)
            out_ref[b, t] = jnp.where(mine, mm(lines, place), 0.0).astype(BF)


def far_kernel(weight_ref, rows_ref, leap_up_ref, leap_down_ref):
    b = pl.program_id(0)
    weight = weight_ref[0, :, :R, :].reshape(2 * R, PAIRS * MOST)
    for d in range(0, rows_ref.shape[3], TILE):
        rows = rows_ref[:, 0, :, d : d + TILE].reshape(PAIRS * MOST, TILE)
        both = mm(weight, rows)
        part = (both[:R] + both[R:]).astype(BF)

        @pl.when(b == 0)
        def _():
            leap_up_ref[:, d : d + TILE] = part

        @pl.when(b == 1)
        def _():
            leap_down_ref[:, d : d + TILE] = part


def combine_kernel(weight_ref, rows_ref, up_ref, down_ref, close_ref):
    half = NH * R - R
    weight = weight_ref[0, :, R:, :].reshape(2 * half, PAIRS * MOST)
    for d in range(0, rows_ref.shape[3], TILE):
        rows = rows_ref[:, 0, :, d : d + TILE].reshape(PAIRS * MOST, TILE)
        both = mm(weight, rows)
        part = (both[:half] + both[half:]).reshape(NH - 1, R, TILE)
        up_ref[0, 0, :, d : d + TILE] = part[0].astype(BF)
        down_ref[0, 0, :, d : d + TILE] = part[1].astype(BF)
        close_ref[0, 0, :, d : d + TILE] = part[2]
        close_ref[1, 0, :, d : d + TILE] = part[3]
        up_ref[1, 0, :, d : d + TILE] = part[4].astype(BF)
        down_ref[1, 0, :, d : d + TILE] = part[5].astype(BF)
        close_ref[2, 0, :, d : d + TILE] = part[6]


def kernel(body, name, shape, dtype, count):
    vmem = pl.BlockSpec(memory_space=pltpu.VMEM)
    return pl.pallas_call(
        body,
        in_specs=[vmem] * count,
        out_specs=vmem,
        out_shape=jax.ShapeDtypeStruct(shape, dtype),
        name=name,
    )


def whole(shape):
    return pl.BlockSpec(shape, lambda b: (0,) * len(shape))


def batch(shape, dim, size=1):
    block = shape[:dim] + (size,) + shape[dim + 1 :]
    return pl.BlockSpec(block, lambda b: (0,) * dim + (b,) + (0,) * (len(shape) - dim - 1))


def shift(value, step):
    return lax.ppermute(value, "zh", [(i, (i + step) % NH) for i in range(NH)])


def shards(hidden, down_weight, routes, route_weight, residual):
    width = down_weight.shape[2]
    slots = hidden.shape[2]
    struct = jax.ShapeDtypeStruct
    packed = kernel(pack_kernel, "pack", (NH, RQ, LANES), F32, 2)(
        routes.transpose(0, 2, 1), route_weight.transpose(0, 2, 1)
    )
    packed = lax.all_to_all(packed, "zh", 0, 0, tiled=True)
    produced = jnp.dot(
        hidden.reshape(B * slots, -1), down_weight[0], preferred_element_type=F32
    ).astype(BF)
    counts = kernel(count_kernel, "count", (M, 1, LANES), F32, 1)(packed)
    counts = jnp.maximum(lax.all_to_all(counts, GROUP, 0, 0, tiled=True), 0.0)
    shape = (M, B, NH * MOST, width)
    sending = pl.pallas_call(
        select_kernel,
        grid=(B,),
        in_specs=[whole(counts.shape), batch(produced.shape, 0, slots)],
        out_specs=batch(shape, 1),
        out_shape=struct(shape, BF),
        name="select",
    )(counts, produced)
    near = lax.all_to_all(sending, GROUP, 0, 0, tiled=True)
    weight = pl.pallas_call(
        weight_kernel,
        in_specs=[
            pl.BlockSpec(memory_space=pltpu.SMEM),
            pl.BlockSpec(memory_space=pltpu.VMEM),
        ],
        out_specs=pl.BlockSpec(memory_space=pltpu.VMEM),
        out_shape=struct((B, 2, NH * R, PAIRS * MOST), BF),
        name="weight",
    )(lax.axis_index("zh").astype(I32).reshape(1), packed)
    one = (R, width)
    both = (2, B, R, width)
    shape = (3, B, R, width)
    inputs = [batch(weight.shape, 0), batch(near.shape, 1)]
    leap_up, leap_down = pl.pallas_call(
        far_kernel,
        grid=(B,),
        in_specs=inputs,
        out_specs=[whole(one)] * 2,
        out_shape=[struct(one, BF)] * 2,
        name="far",
    )(weight, near)
    leap_up, leap_down = shift(leap_up, 2), shift(leap_down, -2)
    up, down, close = pl.pallas_call(
        combine_kernel,
        grid=(B,),
        in_specs=inputs,
        out_specs=[batch(both, 1)] * 2 + [batch(shape, 1)],
        out_shape=[struct(both, BF)] * 2 + [struct(shape, F32)],
        name="combine",
    )(weight, near)
    up, down = shift(up, 1), shift(down, -1)
    above = close[0] + up[0].astype(F32)
    below = close[1] + down[0].astype(F32)
    above = jnp.stack([above[0] + leap_up.astype(F32), above[1]]).astype(BF)
    below = jnp.stack([below[0], below[1] + leap_down.astype(F32)]).astype(BF)
    above, below = shift(above, 2), shift(below, -2)
    base = residual.astype(F32) + close[2] + up[1].astype(F32) + down[1].astype(F32)
    base = lax.optimization_barrier(base)
    return (base + above.astype(F32) + below.astype(F32)).astype(BF)


def solution(mesh):
    fine = Mesh(mesh.devices.reshape(X, NH, NL, C, -1), ("x", "zh", "zl", "c", "dp"))
    ep = ("x", "zh", "zl", "c")
    in_specs = (
        P("dp", ep, None, None),
        P(ep, None, None),
        P("dp", ep, None),
        P("dp", ep, None),
        P("dp", ep, None),
    )
    out_specs = P("dp", ep, None)
    return jax.shard_map(shards, mesh=fine, in_specs=in_specs, out_specs=out_specs, check_vma=False)
```

```python
import jax
import jax.numpy as jnp
from jax import lax
from jax.experimental import pallas as pl
from jax.experimental.pallas import tpu as pltpu
from jax.sharding import Mesh
from jax.sharding import PartitionSpec as P

BF = jnp.bfloat16
F32 = jnp.float32
I32 = jnp.int32

X, Z, C = 4, 16, 2
NL = 2
NH = Z // NL
M = X * NL * C
B, R, MOST = 2, 16, 2
PAIRS = M * NH
TILE = 1024
LANES = 128
RP = LANES // (M * MOST)
RQ = B * R // RP
GROUP = ("x", "zl", "c")


def iota(shape, dim):
    return lax.broadcasted_iota(I32, shape, dim)


def mm(a, b):
    return jnp.dot(a, b, preferred_element_type=F32)


def expert_of(member, high):
    x = member // (NL * C)
    rest = member % (NL * C)
    return (x * NH + high) * (NL * C) + rest


def turned(block):
    eye = (iota((R, R), 0) == iota((R, R), 1)).astype(F32)
    return lax.dot_general(
        eye,
        block,
        (((1,), (1,)), ((), ())),
        precision=lax.Precision.HIGHEST,
        preferred_element_type=F32,
    )


def pack_kernel(routes_ref, weight_ref, out_ref):
    rows = B * R
    routes = jnp.concatenate([turned(routes_ref[b].astype(F32)) for b in range(B)], axis=0)
    weight = jnp.concatenate([turned(weight_ref[b]) for b in range(B)], axis=0)
    row = iota((rows, rows), 0)
    col = iota((rows, rows), 1)
    earlier = ((row // R == col // R) & (col < row)).astype(BF)
    lane = iota((rows, LANES), 1)
    line = iota((rows, LANES), 0)
    member = (lane % (M * MOST)) // MOST
    keep = (line % RP) == lane // (M * MOST)
    for high in range(NH):
        expert = expert_of(member, high).astype(F32)
        total = jnp.zeros((rows, LANES), F32)
        hit = jnp.zeros((rows, LANES), F32)
        for k in range(routes.shape[1]):
            same = routes[:, k : k + 1] == expert
            total = total + jnp.where(same, weight[:, k : k + 1], 0.0)
            hit = hit + jnp.where(same, 1.0, 0.0)
        rank = mm(earlier, hit.astype(BF))
        good = keep & (rank == (lane % MOST).astype(F32))
        value = jnp.where(good, total, 0.0)
        out_ref[high] = jnp.sum(value.reshape(RQ, RP, LANES), axis=1)


def count_kernel(packed_ref, out_ref):
    packed = packed_ref[...].reshape(NH * RQ, LANES)
    used = jnp.where(packed != 0.0, 1.0, 0.0).astype(BF)
    per = RQ // B
    line = iota((LANES, NH * RQ), 1)
    spread = (((line % RQ) // per) * NH + line // RQ == iota((LANES, NH * RQ), 0)).astype(BF)
    by_pair = mm(spread, used).astype(BF)
    pick = (iota((M, LANES), 0) == (iota((M, LANES), 1) % (M * MOST)) // MOST).astype(BF)
    counts = lax.dot_general(
        pick, by_pair, (((1,), (1,)), ((), ())), preferred_element_type=F32
    )
    out_ref[...] = counts[:, None, :]


def select_kernel(counts_ref, rows_ref, out_ref):
    slots = rows_ref.shape[0]
    b = pl.program_id(0)
    counts = counts_ref[:, 0, :].astype(BF)
    dst = iota((PAIRS * MOST, 1), 0)
    src = iota((1, PAIRS), 1)
    s_row = expert_of(dst // (NH * MOST), (dst % (NH * MOST)) // MOST)
    s_col = expert_of(src // NH, src % NH)
    own = iota((M, PAIRS), 0) == iota((M, PAIRS), 1) // NH
    tile = iota((LANES, PAIRS), 0) == iota((LANES, PAIRS), 1) % NH + b * NH
    wide = mm(counts, tile.astype(BF))
    flat = jnp.sum(jnp.where(own, wide, 0.0), axis=0, keepdims=True)
    offset = jnp.sum(jnp.where(s_col < s_row, flat, 0.0), axis=1, keepdims=True)
    at = offset.astype(I32) + dst % MOST
    pick = (at == iota((PAIRS * MOST, slots), 1)).astype(BF)
    for d in range(0, rows_ref.shape[1], TILE):
        out_ref[:, 0, :, d : d + TILE] = (
            mm(pick, rows_ref[:, d : d + TILE]).astype(BF).reshape(M, NH * MOST, TILE)
        )


def weight_kernel(place_ref, packed_ref, out_ref):
    packed = packed_ref[...].reshape(NH * RQ, LANES)
    per = RQ // B
    rows = NH * R
    cols = PAIRS * MOST
    lane = iota((LANES, cols), 0) % (M * MOST)
    col = iota((LANES, cols), 1)
    place = (lane // MOST == col // (NH * MOST)) & (lane % MOST == col % MOST)
    place = place.astype(BF)

    def target(row):
        step = row // R
        far = NH // 2 + jnp.where(step % 2 == 1, -((step + 1) // 2), step // 2)
        return (far + place_ref[0]) % NH

    high = target(iota((rows, 1), 0))
    mine = high == (iota((rows, cols), 1) % (NH * MOST)) // MOST
    row = iota((rows, LANES), 0)
    keep = row % RP == iota((rows, LANES), 1) // (M * MOST)
    inner = (iota((rows, 1), 0) % R) // RP
    first = packed.astype(BF)
    second = (packed - first.astype(F32)).astype(BF)
    for b in range(B):
        line = high * RQ + b * per + inner
        spread = (line == iota((rows, NH * RQ), 1)).astype(BF)
        for t, part in enumerate((first, second)):
            lines = jnp.where(keep, mm(spread, part), 0.0).astype(BF)
            out_ref[b, t] = jnp.where(mine, mm(lines, place), 0.0).astype(BF)


def far_kernel(weight_ref, rows_ref, leap_up_ref, leap_down_ref):
    b = pl.program_id(0)
    weight = weight_ref[0, :, :R, :].reshape(2 * R, PAIRS * MOST)
    for d in range(0, rows_ref.shape[3], TILE):
        rows = rows_ref[:, 0, :, d : d + TILE].reshape(PAIRS * MOST, TILE)
        both = mm(weight, rows)
        part = (both[:R] + both[R:]).astype(BF)

        @pl.when(b == 0)
        def _():
            leap_up_ref[:, d : d + TILE] = part

        @pl.when(b == 1)
        def _():
            leap_down_ref[:, d : d + TILE] = part


def combine_kernel(weight_ref, rows_ref, up_ref, down_ref, above_ref, below_ref, own_ref):
    half = NH * R - R
    weight = weight_ref[0, :, R:, :].reshape(2 * half, PAIRS * MOST)
    for d in range(0, rows_ref.shape[3], TILE):
        rows = rows_ref[:, 0, :, d : d + TILE].reshape(PAIRS * MOST, TILE)
        both = mm(weight, rows)
        part = (both[:half] + both[half:]).reshape(NH - 1, R, TILE)
        up_ref[0, 0, :, d : d + TILE] = part[0].astype(BF)
        down_ref[0, 0, :, d : d + TILE] = part[1].astype(BF)
        above_ref[0, :, d : d + TILE] = part[2]
        below_ref[0, :, d : d + TILE] = part[3]
        up_ref[1, 0, :, d : d + TILE] = part[4].astype(BF)
        down_ref[1, 0, :, d : d + TILE] = part[5].astype(BF)
        own_ref[0, :, d : d + TILE] = part[6]


def kernel(body, name, shape, dtype, count):
    vmem = pl.BlockSpec(memory_space=pltpu.VMEM)
    return pl.pallas_call(
        body,
        in_specs=[vmem] * count,
        out_specs=vmem,
        out_shape=jax.ShapeDtypeStruct(shape, dtype),
        name=name,
    )


def whole(shape):
    return pl.BlockSpec(shape, lambda b: (0,) * len(shape))


def batch(shape, dim, size=1):
    block = shape[:dim] + (size,) + shape[dim + 1 :]
    return pl.BlockSpec(block, lambda b: (0,) * dim + (b,) + (0,) * (len(shape) - dim - 1))


def shift(value, step):
    return lax.ppermute(value, "zh", [(i, (i + step) % NH) for i in range(NH)])


def shards(hidden, down_weight, routes, route_weight, residual):
    width = down_weight.shape[2]
    slots = hidden.shape[2]
    struct = jax.ShapeDtypeStruct
    packed = kernel(pack_kernel, "pack", (NH, RQ, LANES), F32, 2)(
        routes.transpose(0, 2, 1), route_weight.transpose(0, 2, 1)
    )
    packed = lax.all_to_all(packed, "zh", 0, 0, tiled=True)
    produced = jnp.dot(
        hidden.reshape(B * slots, -1), down_weight[0], preferred_element_type=F32
    ).astype(BF)
    counts = kernel(count_kernel, "count", (M, 1, LANES), F32, 1)(packed)
    counts = jnp.maximum(lax.all_to_all(counts, GROUP, 0, 0, tiled=True), 0.0)
    shape = (M, B, NH * MOST, width)
    sending = pl.pallas_call(
        select_kernel,
        grid=(B,),
        in_specs=[whole(counts.shape), batch(produced.shape, 0, slots)],
        out_specs=batch(shape, 1),
        out_shape=struct(shape, BF),
        name="select",
    )(counts, produced)
    near = lax.all_to_all(sending, GROUP, 0, 0, tiled=True)
    weight = pl.pallas_call(
        weight_kernel,
        in_specs=[
            pl.BlockSpec(memory_space=pltpu.SMEM),
            pl.BlockSpec(memory_space=pltpu.VMEM),
        ],
        out_specs=pl.BlockSpec(memory_space=pltpu.VMEM),
        out_shape=struct((B, 2, NH * R, PAIRS * MOST), BF),
        name="weight",
    )(lax.axis_index("zh").astype(I32).reshape(1), packed)
    one = (R, width)
    both = (2, B, R, width)
    plane = (B, R, width)
    inputs = [batch(weight.shape, 0), batch(near.shape, 1)]
    leap_up, leap_down = pl.pallas_call(
        far_kernel,
        grid=(B,),
        in_specs=inputs,
        out_specs=[whole(one)] * 2,
        out_shape=[struct(one, BF)] * 2,
        name="far",
    )(weight, near)
    leap_up, leap_down = shift(leap_up, 2), shift(leap_down, -2)
    up, down, above, below, own = pl.pallas_call(
        combine_kernel,
        grid=(B,),
        in_specs=inputs,
        out_specs=[batch(both, 1)] * 2 + [batch(plane, 0)] * 3,
        out_shape=[struct(both, BF)] * 2 + [struct(plane, F32)] * 3,
        name="combine",
    )(weight, near)
    up, down = shift(up, 1), shift(down, -1)
    above = above + up[0].astype(F32)
    below = below + down[0].astype(F32)
    above = jnp.stack([above[0] + leap_up.astype(F32), above[1]]).astype(BF)
    below = jnp.stack([below[0], below[1] + leap_down.astype(F32)]).astype(BF)
    above, below = shift(above, 2), shift(below, -2)
    base = residual.astype(F32) + own + up[1].astype(F32) + down[1].astype(F32)
    base = lax.optimization_barrier(base)
    return (base + above.astype(F32) + below.astype(F32)).astype(BF)


def solution(mesh):
    fine = Mesh(mesh.devices.reshape(X, NH, NL, C, -1), ("x", "zh", "zl", "c", "dp"))
    ep = ("x", "zh", "zl", "c")
    in_specs = (
        P("dp", ep, None, None),
        P(ep, None, None),
        P("dp", ep, None),
        P("dp", ep, None),
        P("dp", ep, None),
    )
    out_specs = P("dp", ep, None)
    return jax.shard_map(shards, mesh=fine, in_specs=in_specs, out_specs=out_specs, check_vma=False)
```

```python
import jax
import jax.numpy as jnp
from jax import lax
from jax.experimental import pallas as pl
from jax.experimental.pallas import tpu as pltpu
from jax.sharding import Mesh
from jax.sharding import PartitionSpec as P

BF = jnp.bfloat16
F32 = jnp.float32
I32 = jnp.int32

X, Z, C = 4, 16, 2
NL = 2
NH = Z // NL
M = X * NL * C
B, R, MOST = 2, 16, 2
PAIRS = M * NH
TILE = 1024
LANES = 128
RP = LANES // (M * MOST)
RQ = B * R // RP
GROUP = ("x", "zl", "c")


def iota(shape, dim):
    return lax.broadcasted_iota(I32, shape, dim)


def mm(a, b):
    return jnp.dot(a, b, preferred_element_type=F32)


def expert_of(member, high):
    x = member // (NL * C)
    rest = member % (NL * C)
    return (x * NH + high) * (NL * C) + rest


def turned(block):
    return block.T


def pack_kernel(routes_ref, weight_ref, out_ref):
    rows = B * R
    routes = jnp.concatenate([turned(routes_ref[b].astype(F32)) for b in range(B)], axis=0)
    weight = jnp.concatenate([turned(weight_ref[b]) for b in range(B)], axis=0)
    row = iota((rows, rows), 0)
    col = iota((rows, rows), 1)
    earlier = ((row // R == col // R) & (col < row)).astype(BF)
    lane = iota((rows, LANES), 1)
    line = iota((rows, LANES), 0)
    member = (lane % (M * MOST)) // MOST
    keep = (line % RP) == lane // (M * MOST)
    for high in range(NH):
        expert = expert_of(member, high).astype(F32)
        total = jnp.zeros((rows, LANES), F32)
        hit = jnp.zeros((rows, LANES), F32)
        for k in range(routes.shape[1]):
            same = routes[:, k : k + 1] == expert
            total = total + jnp.where(same, weight[:, k : k + 1], 0.0)
            hit = hit + jnp.where(same, 1.0, 0.0)
        rank = mm(earlier, hit.astype(BF))
        good = keep & (rank == (lane % MOST).astype(F32))
        value = jnp.where(good, total, 0.0)
        out_ref[high] = jnp.sum(value.reshape(RQ, RP, LANES), axis=1)


def count_kernel(packed_ref, out_ref):
    packed = packed_ref[...].reshape(NH * RQ, LANES)
    used = jnp.where(packed != 0.0, 1.0, 0.0).astype(BF)
    per = RQ // B
    line = iota((LANES, NH * RQ), 1)
    spread = (((line % RQ) // per) * NH + line // RQ == iota((LANES, NH * RQ), 0)).astype(BF)
    by_pair = mm(spread, used).astype(BF)
    pick = (iota((M, LANES), 0) == (iota((M, LANES), 1) % (M * MOST)) // MOST).astype(BF)
    counts = lax.dot_general(
        pick, by_pair, (((1,), (1,)), ((), ())), preferred_element_type=F32
    )
    out_ref[...] = counts[:, None, :]


def select_kernel(counts_ref, rows_ref, out_ref):
    slots = rows_ref.shape[0]
    b = pl.program_id(0)
    counts = counts_ref[:, 0, :].astype(BF)
    dst = iota((PAIRS * MOST, 1), 0)
    src = iota((1, PAIRS), 1)
    s_row = expert_of(dst // (NH * MOST), (dst % (NH * MOST)) // MOST)
    s_col = expert_of(src // NH, src % NH)
    own = iota((M, PAIRS), 0) == iota((M, PAIRS), 1) // NH
    tile = iota((LANES, PAIRS), 0) == iota((LANES, PAIRS), 1) % NH + b * NH
    wide = mm(counts, tile.astype(BF))
    flat = jnp.sum(jnp.where(own, wide, 0.0), axis=0, keepdims=True)
    offset = jnp.sum(jnp.where(s_col < s_row, flat, 0.0), axis=1, keepdims=True)
    at = offset.astype(I32) + dst % MOST
    pick = (at == iota((PAIRS * MOST, slots), 1)).astype(BF)
    for d in range(0, rows_ref.shape[1], TILE):
        out_ref[:, 0, :, d : d + TILE] = (
            mm(pick, rows_ref[:, d : d + TILE]).astype(BF).reshape(M, NH * MOST, TILE)
        )


def weight_kernel(place_ref, packed_ref, out_ref):
    packed = packed_ref[...].reshape(NH * RQ, LANES)
    per = RQ // B
    rows = NH * R
    cols = PAIRS * MOST
    lane = iota((LANES, cols), 0) % (M * MOST)
    col = iota((LANES, cols), 1)
    place = (lane // MOST == col // (NH * MOST)) & (lane % MOST == col % MOST)
    place = place.astype(BF)

    def target(row):
        step = row // R
        far = NH // 2 + jnp.where(step % 2 == 1, -((step + 1) // 2), step // 2)
        return (far + place_ref[0]) % NH

    high = target(iota((rows, 1), 0))
    mine = high == (iota((rows, cols), 1) % (NH * MOST)) // MOST
    row = iota((rows, LANES), 0)
    keep = row % RP == iota((rows, LANES), 1) // (M * MOST)
    inner = (iota((rows, 1), 0) % R) // RP
    first = packed.astype(BF)
    second = (packed - first.astype(F32)).astype(BF)
    for b in range(B):
        line = high * RQ + b * per + inner
        spread = (line == iota((rows, NH * RQ), 1)).astype(BF)
        for t, part in enumerate((first, second)):
            lines = jnp.where(keep, mm(spread, part), 0.0).astype(BF)
            out_ref[b, t] = jnp.where(mine, mm(lines, place), 0.0).astype(BF)


def far_kernel(weight_ref, rows_ref, leap_up_ref, leap_down_ref):
    b = pl.program_id(0)
    weight = weight_ref[0, :, :R, :].reshape(2 * R, PAIRS * MOST)
    for d in range(0, rows_ref.shape[3], TILE):
        rows = rows_ref[:, 0, :, d : d + TILE].reshape(PAIRS * MOST, TILE)
        both = mm(weight, rows)
        part = (both[:R] + both[R:]).astype(BF)

        @pl.when(b == 0)
        def _():
            leap_up_ref[:, d : d + TILE] = part

        @pl.when(b == 1)
        def _():
            leap_down_ref[:, d : d + TILE] = part


def combine_kernel(weight_ref, rows_ref, up_ref, down_ref, above_ref, below_ref, own_ref):
    half = NH * R - R
    weight = weight_ref[0, :, R:, :].reshape(2 * half, PAIRS * MOST)
    for d in range(0, rows_ref.shape[3], TILE):
        rows = rows_ref[:, 0, :, d : d + TILE].reshape(PAIRS * MOST, TILE)
        both = mm(weight, rows)
        part = (both[:half] + both[half:]).reshape(NH - 1, R, TILE)
        up_ref[0, 0, :, d : d + TILE] = part[0].astype(BF)
        down_ref[0, 0, :, d : d + TILE] = part[1].astype(BF)
        above_ref[0, :, d : d + TILE] = part[2]
        below_ref[0, :, d : d + TILE] = part[3]
        up_ref[1, 0, :, d : d + TILE] = part[4].astype(BF)
        down_ref[1, 0, :, d : d + TILE] = part[5].astype(BF)
        own_ref[0, :, d : d + TILE] = part[6]


def kernel(body, name, shape, dtype, count):
    vmem = pl.BlockSpec(memory_space=pltpu.VMEM)
    return pl.pallas_call(
        body,
        in_specs=[vmem] * count,
        out_specs=vmem,
        out_shape=jax.ShapeDtypeStruct(shape, dtype),
        name=name,
    )


def whole(shape):
    return pl.BlockSpec(shape, lambda b: (0,) * len(shape))


def batch(shape, dim, size=1):
    block = shape[:dim] + (size,) + shape[dim + 1 :]
    return pl.BlockSpec(block, lambda b: (0,) * dim + (b,) + (0,) * (len(shape) - dim - 1))


def shift(value, step):
    return lax.ppermute(value, "zh", [(i, (i + step) % NH) for i in range(NH)])


def shards(hidden, down_weight, routes, route_weight, residual):
    width = down_weight.shape[2]
    slots = hidden.shape[2]
    struct = jax.ShapeDtypeStruct
    packed = kernel(pack_kernel, "pack", (NH, RQ, LANES), F32, 2)(
        routes.transpose(0, 2, 1), route_weight.transpose(0, 2, 1)
    )
    packed = lax.all_to_all(packed, "zh", 0, 0, tiled=True)
    produced = jnp.dot(
        hidden.reshape(B * slots, -1), down_weight[0], preferred_element_type=F32
    ).astype(BF)
    counts = kernel(count_kernel, "count", (M, 1, LANES), F32, 1)(packed)
    counts = jnp.maximum(lax.all_to_all(counts, GROUP, 0, 0, tiled=True), 0.0)
    shape = (M, B, NH * MOST, width)
    sending = pl.pallas_call(
        select_kernel,
        grid=(B,),
        in_specs=[whole(counts.shape), batch(produced.shape, 0, slots)],
        out_specs=batch(shape, 1),
        out_shape=struct(shape, BF),
        name="select",
    )(counts, produced)
    near = lax.all_to_all(sending, GROUP, 0, 0, tiled=True)
    weight = pl.pallas_call(
        weight_kernel,
        in_specs=[
            pl.BlockSpec(memory_space=pltpu.SMEM),
            pl.BlockSpec(memory_space=pltpu.VMEM),
        ],
        out_specs=pl.BlockSpec(memory_space=pltpu.VMEM),
        out_shape=struct((B, 2, NH * R, PAIRS * MOST), BF),
        name="weight",
    )(lax.axis_index("zh").astype(I32).reshape(1), packed)
    one = (R, width)
    both = (2, B, R, width)
    plane = (B, R, width)
    inputs = [batch(weight.shape, 0), batch(near.shape, 1)]
    leap_up, leap_down = pl.pallas_call(
        far_kernel,
        grid=(B,),
        in_specs=inputs,
        out_specs=[whole(one)] * 2,
        out_shape=[struct(one, BF)] * 2,
        name="far",
    )(weight, near)
    leap_up, leap_down = shift(leap_up, 2), shift(leap_down, -2)
    up, down, above, below, own = pl.pallas_call(
        combine_kernel,
        grid=(B,),
        in_specs=inputs,
        out_specs=[batch(both, 1)] * 2 + [batch(plane, 0)] * 3,
        out_shape=[struct(both, BF)] * 2 + [struct(plane, F32)] * 3,
        name="combine",
    )(weight, near)
    up, down = shift(up, 1), shift(down, -1)
    above = above + up[0].astype(F32)
    below = below + down[0].astype(F32)
    above = jnp.stack([above[0] + leap_up.astype(F32), above[1]]).astype(BF)
    below = jnp.stack([below[0], below[1] + leap_down.astype(F32)]).astype(BF)
    above, below = shift(above, 2), shift(below, -2)
    base = residual.astype(F32) + own + up[1].astype(F32) + down[1].astype(F32)
    base = lax.optimization_barrier(base)
    return (base + above.astype(F32) + below.astype(F32)).astype(BF)


def solution(mesh):
    fine = Mesh(mesh.devices.reshape(X, NH, NL, C, -1), ("x", "zh", "zl", "c", "dp"))
    ep = ("x", "zh", "zl", "c")
    in_specs = (
        P("dp", ep, None, None),
        P(ep, None, None),
        P("dp", ep, None),
        P("dp", ep, None),
        P("dp", ep, None),
    )
    out_specs = P("dp", ep, None)
    return jax.shard_map(shards, mesh=fine, in_specs=in_specs, out_specs=out_specs, check_vma=False)
```
